128 devices in a mesh: rows: 32 (over z, x_lo, y), bands: 4 (over x_hi, core).
Axes of the slice: x: 4 (x_hi: 2, x_lo: 2; x = x_hi * 2 + x_lo), y: 4, z: 4, core: 2. Of those that a mesh axis runs over, the one named last changes fastest.
Arguments:
- vectors: float32 [32768, 1024], P('rows', 'bands'), may hold values from -6 to 6
- local_blocks: float32 [256, 6, 128, 128], P('rows'), may hold values from -0.078125 to 0.078125
- local_cols: int32 [256, 6], P('rows'), may hold values from 0 to 7
- coupling_blocks: float32 [3, 256, 2, 128, 128], P(None, 'rows'), may hold values from -0.078125 to 0.078125
- coupling_cols: int32 [3, 256, 2], replicated, may hold values from 0 to 7
- partners: int32 [3, 32], replicated, may hold values from 0 to 31, as said below
- bounds: float32 [3], replicated, may hold values from -2.8 to 2.8, as said below
- rotation: float32 [1024, 1024], replicated, may hold values from -1 to 1
Outputs:
- rotated: float32 [32768, 1024], P('rows', 'bands')
The draws below stay inside these ranges and needn't reach their ends.
Inputs may be any that keep to these rules, and one draw needn't show every extreme that they name: For each colour c there is a bit number b_c, with the three b_c distinct, such that partners[c, i] = i XOR 2 ** b_c for every row shard i. `local_cols`: local block columns count inside the row shard itself. `coupling_cols`: coupling block columns count inside the partner shard of that colour. bounds[0] < bounds[1] < bounds[2].
All inputs are finite; a program needn't handle non-finite values.
Results may differ from the reference program's by a relative error of at most 0.0003.
Values sent between devices are 32-bit elements; how exact they have to be, the bound alone decides.
A program may use at most 128 MiB of HBM per device.

```python
import jax
import jax.numpy as jnp
from jax import lax

BLK = 128
KL = 6
KC = 2
NB = 1024
ROWS_DEV = 1024
TOTAL_ROWS = 32768
NBLK = 256
N_ROWS = 32


def draw_partners(key, part):
    bit_total = N_ROWS.bit_length() - 1
    chosen = jax.random.permutation(jax.random.fold_in(key, 11), bit_total)[:3].astype(jnp.int32)
    masks = jnp.left_shift(jnp.ones((3,), jnp.int32), chosen)
    shard_ids = jnp.arange(N_ROWS, dtype=jnp.int32)
    return jnp.bitwise_xor(shard_ids[None, :], masks[:, None]).astype(jnp.int32)


def draw_bounds(key, part):
    sub_keys = jax.random.split(jax.random.fold_in(key, 5), 3)
    lowest = jax.random.uniform(sub_keys[0], (), jnp.float32, -2.8, -2.3)
    lower = jax.random.uniform(sub_keys[1], (), jnp.float32, -1.2, -0.6)
    upper = jax.random.uniform(sub_keys[2], (), jnp.float32, 2.2, 2.8)
    return jnp.stack([lowest, lower, upper])


def draw_rotation(key, part):
    inner_key = jax.random.fold_in(key, 7)
    base = jax.random.normal(inner_key, (NB, NB), jnp.float32)
    orthogonal, upper_part = jnp.linalg.qr(base)
    return orthogonal.astype(jnp.float32)


def set_ends(entries, key, least, top_value):
    place = [jax.random.randint(jax.random.fold_in(key, axis), (), 0, length) for axis, length in enumerate(entries.shape)]
    main_axis = entries.shape.index(max(entries.shape))
    next_to = place[:main_axis] + [(place[main_axis] + 1) % entries.shape[main_axis]] + place[main_axis + 1:]
    return entries.at[tuple(place)].set(least).at[tuple(next_to)].set(top_value)


def levels(rng, shape, pieces, low, high):
    loudness = 1.0
    for position, blocks in pieces:
        heights = jax.random.uniform(jax.random.fold_in(jax.random.fold_in(rng, 6), position), (blocks,), jnp.float32, low / len(pieces), high / len(pieces))
        loudness = loudness * jnp.repeat(jnp.exp(heights), shape[position] // blocks).reshape((-1,) + (1,) * (len(shape) - 1 - position))
    return loudness


def centred(stream_key, dims, deviation, most, pieces=(), kind=jnp.bfloat16):
    level = levels(stream_key, dims, pieces, -0.22, 0.18) if pieces else 1.0
    values = jax.random.normal(stream_key, dims, jnp.float32) * deviation * level
    return jnp.minimum(jnp.maximum(values, -most), most).astype(kind)


def setup_inputs(seed: int = 0) -> dict:
    keys = jax.random.split(jax.random.key(seed), 9)
    return {
        "vectors": centred(keys[0], (TOTAL_ROWS, NB), 1.0, 6.0, ((0, 32), (1, 4)), jnp.float32),
        "local_blocks": centred(keys[1], (NBLK, KL, BLK, BLK), (4 * BLK * (KL + 3 * KC)) ** -0.5, 0.078125, ((0, 32),), jnp.float32),
        "local_cols": set_ends(jax.random.randint(keys[2], (NBLK, KL), 0, ROWS_DEV // BLK), jax.random.fold_in(keys[2], 1), 0, (ROWS_DEV // BLK) - 1).astype(jnp.int32),
        "coupling_blocks": centred(keys[3], (3, NBLK, KC, BLK, BLK), (4 * BLK * (KL + 3 * KC)) ** -0.5, 0.078125, ((1, 32),), jnp.float32),
        "coupling_cols": set_ends(jax.random.randint(keys[4], (3, NBLK, KC), 0, ROWS_DEV // BLK), jax.random.fold_in(keys[4], 1), 0, (ROWS_DEV // BLK) - 1).astype(jnp.int32),
        "partners": draw_partners(jax.random.fold_in(keys[8], 71), 0),
        "bounds": draw_bounds(jax.random.fold_in(keys[8], 71), 0),
        "rotation": draw_rotation(jax.random.fold_in(keys[8], 71), 0),
    }


precise = lax.Precision.HIGHEST

def forward(blocks, block_cols, source):
    picked = jnp.take(source, block_cols, axis=0)
    return jnp.einsum('akij,akjw->aiw', blocks, picked, precision=precise)

def backward(blocks, block_cols, source, block_count):
    products = jnp.einsum('akij,aiw->akjw', blocks, source, precision=precise)
    targets = jnp.arange(block_count, dtype=jnp.int32)
    onehot = (block_cols[:, :, None] == targets[None, None, :]).astype(jnp.float32)
    return jnp.einsum('akc,akjw->cjw', onehot, products, precision=precise)

def apply_hamiltonian(current, local_blocks, local_cols, coupling_blocks, coupling_cols, partners):
    shard_count = partners.shape[1]
    block_count = ROWS_DEV // BLK
    shards_view = current.reshape(shard_count, block_count, BLK, NB)
    local_view = local_blocks.reshape(shard_count, block_count, KL, BLK, BLK)
    local_index = local_cols.reshape(shard_count, block_count, KL)
    couple_view = coupling_blocks.reshape(3, shard_count, block_count, KC, BLK, BLK)
    couple_index = coupling_cols.reshape(3, shard_count, block_count, KC)

    def one_shard(shard):
        own = shards_view[shard]
        result = forward(local_view[shard], local_index[shard], own)
        result = result + backward(local_view[shard], local_index[shard], own, block_count)
        for colour in range(3):
            mate = partners[colour, shard]
            mate_field = shards_view[mate]
            result = result + forward(couple_view[colour, shard], couple_index[colour, shard], mate_field)
            result = result + backward(couple_view[colour, mate], couple_index[colour, mate], mate_field, block_count)
        return result
    outcome = lax.map(one_shard, jnp.arange(shard_count, dtype=jnp.int32))
    return outcome.reshape(current.shape)

def reference(vectors, local_blocks, local_cols, coupling_blocks, coupling_cols, partners, bounds, rotation):
    lowest, lower, upper = (bounds[0], bounds[1], bounds[2])
    half_width = (upper - lower) / 2.0
    centre = (upper + lower) / 2.0
    sigma_one = half_width / (lowest - centre)
    sigma_two = 1.0 / (2.0 / sigma_one - sigma_one)

    def apply_field(current):
        return apply_hamiltonian(current, local_blocks, local_cols, coupling_blocks, coupling_cols, partners)
    filtered = (apply_field(vectors) - centre * vectors) * (sigma_one / half_width)
    second = (apply_field(filtered) - centre * filtered) * (2.0 * sigma_two / half_width) - sigma_one * sigma_two * vectors
    return jnp.dot(second.astype(jnp.float32), rotation.astype(jnp.float32), precision=precise, preferred_element_type=jnp.float32)
```

```python
import functools
import itertools

import jax
import jax.numpy as jnp
from jax import lax
from jax.experimental import pallas as pl
from jax.experimental.pallas import tpu as pltpu
from jax.sharding import PartitionSpec as P

MESH = pl.DeviceIdType.MESH
f32, bf16 = jnp.float32, jnp.bfloat16
ROWS, WIDTH, BLK = 1024, 256, 128
BC = ROWS // BLK
KL, KC = 6, 2
CH = 8
TR = 256
COMBOS = sorted(itertools.combinations(range(5), 3), key=lambda bits: sum(1 << b for b in bits))
TOTALS = [sum(1 << b for b in bits) for bits in COMBOS]


def flip(index, mask):
    bit, out = 1, index
    while bit <= mask:
        if mask & bit:
            out = out + bit * (1 - 2 * lax.rem(lax.div(index, bit), 2))
        bit *= 2
    return out


def dot(a, b):
    return jnp.dot(a, b, preferred_element_type=f32)


def split(x):
    hi = x.astype(bf16)
    return hi, (x - hi.astype(f32)).astype(bf16)


def rows_of(m, size):
    return pl.ds(pl.multiple_of(m * size, size), size)


def kernel(
    bits, local_cols, couple_cols, partners, bounds, v_hbm, local_hbm, couple_hbm, rot_hbm, out_hbm,
    v_own, v_mate, f_own, f_mate, acc, s_own, s_other, own_blocks, turned, couple, outgoing,
    mate_blocks, h_local, h_couple, src_hi, src_lo, mate_hi, mate_lo, rot, rot_hi, rot_lo, out_v,
    in_sem, rot_sem, out_sem, v_send, v_recv, f_send, f_recv, b_send, b_recv, bf_send, bf_recv,
    g_send, g_recv,
):
    masks = [1 << b for b in bits]
    row, band = lax.axis_index("rows"), lax.axis_index("bands")
    core = lax.rem(band, 2)
    relay = None
    for low, high in ((0, 1), (3, 4)):
        if low in bits and high in bits:
            relay = (bits.index(low), bits.index(high))
    direct = [p for p in range(3) if relay is None or p != relay[1]]
    mates = [(flip(row, m), band) for m in masks]
    twin = (row, flip(band, 1))
    across = (row, flip(band, 2))
    peers = mates + [twin, across]
    if relay is not None:
        onward = (flip(row, masks[relay[0]] | masks[relay[1]]), band)
        peers.append(onward)

    def remote(src, dst, send, recv, to):
        return pltpu.make_async_remote_copy(
            src_ref=src, dst_ref=dst, send_sem=send, recv_sem=recv, device_id=to, device_id_type=MESH
        )

    loads = [
        pltpu.make_async_copy(couple_hbm, couple, in_sem.at[0]),
        pltpu.make_async_copy(local_hbm, own_blocks, in_sem.at[1]),
        pltpu.make_async_copy(v_hbm, v_own, in_sem.at[2]),
    ]
    for load in loads:
        load.start()
    rot_loads = []
    for g in range(4):
        piece = rot_hbm.at[rows_of(flip(band, g), WIDTH), rows_of(band, WIDTH)]
        rot_loads.append(pltpu.make_async_copy(piece, rot.at[pl.ds(g * WIDTH, WIDTH)], rot_sem.at[g]))
        rot_loads[-1].start()

    barrier = pltpu.get_barrier_semaphore()
    for peer in peers:
        pl.semaphore_signal(barrier, inc=1, device_id=peer, device_id_type=MESH)
    pl.semaphore_wait(barrier, len(peers))

    def exchange(src, mate_buf, send, recv):
        def chunk(p, c, to, source):
            rs = rows_of(c, BLK)
            return remote(source.at[rs], mate_buf.at[p, rs], send.at[p, c], recv.at[p, c], to)

        def start(c):
            for p in direct:
                chunk(p, c, mates[p], src).start()

        def pass_on(c):
            if relay is not None:
                near, far = relay
                chunk(near, c, mates[near], src).wait_recv()
                chunk(far, c, onward, mate_buf.at[near]).start()

        def arrive(c):
            for p in range(3):
                if relay is None or p != relay[0]:
                    chunk(p, c, mates[p], src).wait_recv()

        def drain():
            for c in range(CH):
                for p in range(3):
                    if p in direct:
                        chunk(p, c, mates[p], src).wait_send()
                    else:
                        chunk(p, c, onward, mate_buf.at[relay[0]]).wait_send()

        return start, pass_on, arrive, drain

    v_start, v_pass, v_arrive, v_drain = exchange(v_hbm, v_mate, v_send, v_recv)
    f_start, f_pass, f_arrive, f_drain = exchange(f_own, f_mate, f_send, f_recv)

    v_start(0)
    v_start(1)

    colours = []
    for m in masks:
        colour = jnp.int32(0)
        for c in (1, 2):
            colour = colour + jnp.where(partners[c, 0] == m, c, 0)
        colours.append(colour)

    half = BC * KC // 2
    first = core * half
    loads[0].wait()
    blocks = []
    for p in range(3):
        @pl.loop(0, half // 4)
        def _(q, p=p):
            for u in range(4):
                outgoing[p, q * 4 + u] = couple[colours[p], first + q * 4 + u]

        blocks.append(
            remote(outgoing.at[p], mate_blocks.at[p, pl.ds(first, half)], b_send.at[p], b_recv.at[p], mates[p])
        )
        blocks[-1].start()
    for c in range(2, CH):
        v_start(c)

    def turn(source, count):
        @pl.loop(0, count // 8)
        def _(q):
            for u in range(8):
                turned[q * 8 + u] = source[q * 8 + u].T

    def one_if(flag):
        return jnp.where(flag, 1.0, 0.0).astype(f32)

    loads[1].wait()
    turn(own_blocks, BC * KL)

    @pl.loop(0, BC)
    def _(i):
        rs = rows_of(i, BLK)
        for j in range(BC):
            total = None
            for k in range(KL):
                term = own_blocks[i * KL + k] * one_if(local_cols[i, k] == j)
                total = term if total is None else total + term
            for k in range(KL):
                total = total + turned[j * KL + k] * one_if(local_cols[j, k] == i)
            hi, lo = split(total)
            h_local[rs, j * BLK:(j + 1) * BLK] = hi
            h_local[rs, ROWS + j * BLK:ROWS + (j + 1) * BLK] = lo

    v_pass(0)
    v_pass(1)

    def local_product():
        for m in range(ROWS // 512):
            rs = slice(m * 512, (m + 1) * 512)
            acc[rs] = (
                dot(h_local[rs, :ROWS], src_hi[...])
                + dot(h_local[rs, ROWS:], src_hi[...])
                + dot(h_local[rs, :ROWS], src_lo[...])
            )

    loads[2].wait()
    for c in range(4):
        rs = slice(c * TR, (c + 1) * TR)
        src_hi[rs], src_lo[rs] = split(v_own[rs])
    local_product()

    forwards = []
    for p in range(3):
        blocks[p].wait_recv()
        span = mate_blocks.at[p, pl.ds(first, half)]
        forwards.append(remote(span, span, bf_send.at[p], bf_recv.at[p], twin))
        forwards[-1].start()
    for p in range(3):
        forwards[p].wait_recv()
        turn(mate_blocks.at[p], BC * KC)
        mate_row = mates[p][0]

        @pl.loop(0, BC)
        def _(i, p=p, mate_row=mate_row):
            rs = rows_of(i, BLK)
            for j in range(BC):
                total = None
                for k in range(KC):
                    flag = one_if(couple_cols[colours[p], row * BC + i, k] == j)
                    term = couple[colours[p], i * KC + k] * flag
                    total = term if total is None else total + term
                for k in range(KC):
                    flag = one_if(couple_cols[colours[p], mate_row * BC + j, k] == i)
                    total = total + turned[j * KC + k] * flag
                hi, lo = split(total)
                at = p * TR + (j % 2) * BLK
                h_couple[j // 2, rs, at:at + BLK] = hi
                h_couple[j // 2, rs, 3 * TR + at:3 * TR + at + BLK] = lo

        v_pass(2 + p)

    def couple_product(kc, rs):
        return (
            dot(h_couple[kc, rs, :3 * TR], mate_hi[...])
            + dot(h_couple[kc, rs, 3 * TR:], mate_hi[...])
            + dot(h_couple[kc, rs, :3 * TR], mate_lo[...])
        )

    def gather(mate_buf, passed, pass_on, arrive, finish):
        for kc in range(4):
            for c in (2 * kc, 2 * kc + 1):
                if c >= passed:
                    pass_on(c)
            for c in (2 * kc, 2 * kc + 1):
                arrive(c)
            for p in range(3):
                hi, lo = split(mate_buf[p, kc * TR:(kc + 1) * TR])
                mate_hi[p * TR:(p + 1) * TR] = hi
                mate_lo[p * TR:(p + 1) * TR] = lo
            if kc < 3:
                for m in range(ROWS // 512):
                    rs = slice(m * 512, (m + 1) * 512)
                    acc[rs] += couple_product(kc, rs)
            else:
                for m in range(ROWS // TR):
                    rs = slice(m * TR, (m + 1) * TR)
                    finish(m, rs, acc[rs] + couple_product(kc, rs))

    wide = (1, WIDTH)
    lowest, lower, upper = (jnp.full(wide, bounds[i], f32) for i in range(3))
    half_width = (upper - lower) / 2.0
    centre = (upper + lower) / 2.0
    sigma_one = half_width / (lowest - centre)
    sigma_two = 1.0 / (2.0 / sigma_one - sigma_one)

    def finish_first(m, rs, total):
        filtered = (total - centre * v_own[rs]) * (sigma_one / half_width)
        f_own[rs] = filtered
        f_start(2 * m)
        f_start(2 * m + 1)
        src_hi[rs], src_lo[rs] = split(filtered)

    gather(v_mate, 5, v_pass, v_arrive, finish_first)

    local_product()
    for load in rot_loads:
        load.wait()
    for g in range(4):
        rs = slice(g * WIDTH, (g + 1) * WIDTH)
        rot_hi[rs], rot_lo[rs] = split(rot[rs])

    def hand(kind, m):
        rs = rows_of(m, TR)
        source = s_other.at[1] if kind == 2 else s_own
        return remote(
            source.at[rs], s_other.at[kind, rs], g_send.at[kind, m], g_recv.at[kind, m], across if kind == 1 else twin
        )

    def finish_second(m, rs, total):
        second = (total - centre * f_own[rs]) * (2.0 * sigma_two / half_width) - sigma_one * sigma_two * v_own[rs]
        s_own[rs] = second
        hand(1, m).start()
        hand(0, m).start()

    gather(f_mate, 0, f_pass, f_arrive, finish_second)

    stores = []
    for m in range(ROWS // TR):
        rs = slice(m * TR, (m + 1) * TR)
        hand(1, m).wait_recv()
        hand(2, m).start()
        hand(0, m).wait_recv()
        total = None
        for g in range(3):
            part = s_own[rs] if g == 0 else s_other[g - 1, rs]
            hi, lo = split(part)
            gs = slice(g * WIDTH, (g + 1) * WIDTH)
            term = dot(hi, rot_hi[gs]) + dot(lo, rot_hi[gs]) + dot(hi, rot_lo[gs])
            total = term if total is None else total + term
        hand(2, m).wait_recv()
        hi, lo = split(s_other[2, rs])
        gs = slice(3 * WIDTH, 4 * WIDTH)
        out_v[rs] = total + (dot(hi, rot_hi[gs]) + dot(lo, rot_hi[gs]) + dot(hi, rot_lo[gs]))
        stores.append(pltpu.make_async_copy(out_v.at[pl.ds(m * TR, TR)], out_hbm.at[pl.ds(m * TR, TR)], out_sem.at[m]))
        stores[-1].start()

    v_drain()
    f_drain()
    for p in range(3):
        blocks[p].wait_send()
        forwards[p].wait_send()
    for m in range(ROWS // TR):
        for kind in range(3):
            hand(kind, m).wait_send()
        stores[m].wait()


def fused(bits, number):
    dma = pltpu.SemaphoreType.DMA
    scratch = [
        pltpu.VMEM((ROWS, WIDTH), f32),
        pltpu.VMEM((3, ROWS, WIDTH), f32),
        pltpu.VMEM((ROWS, WIDTH), f32),
        pltpu.VMEM((3, ROWS, WIDTH), f32),
        pltpu.VMEM((ROWS, WIDTH), f32),
        pltpu.VMEM((ROWS, WIDTH), f32),
        pltpu.VMEM((3, ROWS, WIDTH), f32),
        pltpu.VMEM((BC * KL, BLK, BLK), f32),
        pltpu.VMEM((BC * KL, BLK, BLK), f32),
        pltpu.VMEM((3, BC * KC, BLK, BLK), f32),
        pltpu.VMEM((3, BC * KC // 2, BLK, BLK), f32),
        pltpu.VMEM((3, BC * KC, BLK, BLK), f32),
        pltpu.VMEM((ROWS, 2 * ROWS), bf16),
        pltpu.VMEM((4, ROWS, 6 * TR), bf16),
        pltpu.VMEM((ROWS, WIDTH), bf16),
        pltpu.VMEM((ROWS, WIDTH), bf16),
        pltpu.VMEM((3 * TR, WIDTH), bf16),
        pltpu.VMEM((3 * TR, WIDTH), bf16),
        pltpu.VMEM((4 * WIDTH, WIDTH), f32),
        pltpu.VMEM((4 * WIDTH, WIDTH), bf16),
        pltpu.VMEM((4 * WIDTH, WIDTH), bf16),
        pltpu.VMEM((ROWS, WIDTH), f32),
        dma((3,)), dma((4,)), dma((4,)),
        dma((3, CH)), dma((3, CH)), dma((3, CH)), dma((3, CH)),
        dma((3,)), dma((3,)), dma((3,)), dma((3,)),
        dma((3, 4)), dma((3, 4)),
    ]
    smem, hbm = pl.BlockSpec(memory_space=pltpu.SMEM), pl.BlockSpec(memory_space=pl.ANY)
    return pl.pallas_call(
        functools.partial(kernel, bits),
        out_shape=jax.ShapeDtypeStruct((ROWS, WIDTH), f32),
        in_specs=[smem] * 4 + [hbm] * 4,
        out_specs=hbm,
        scratch_shapes=scratch,
        compiler_params=pltpu.CompilerParams(
            collective_id=number, has_side_effects=True, vmem_limit_bytes=60 << 20
        ),
        name="filter_" + "".join(map(str, bits)),
    )


def local(
    vectors, local_blocks, local_cols, coupling_blocks, coupling_cols, partners, bounds, rotation
):
    total = partners[0, 0] + partners[1, 0] + partners[2, 0]
    index = sum((total > t).astype(jnp.int32) for t in TOTALS[:-1])
    return lax.switch(
        index,
        [fused(bits, number) for number, bits in enumerate(COMBOS)],
        local_cols, coupling_cols, partners, bounds, vectors,
        local_blocks.reshape(BC * KL, BLK, BLK),
        coupling_blocks.reshape(3, BC * KC, BLK, BLK),
        rotation,
    )


def solution(mesh):
    in_specs = (
        P("rows", "bands"),
        P("rows", None, None, None),
        P("rows", None),
        P(None, "rows", None, None, None),
        P(),
        P(),
        P(),
        P(),
    )
    out_specs = P("rows", "bands")
    return jax.shard_map(local, mesh=mesh, in_specs=in_specs, out_specs=out_specs, check_vma=False)
```

```python
import functools
import itertools

import jax
import jax.numpy as jnp
from jax import lax
from jax.experimental import pallas as pl
from jax.experimental.pallas import tpu as pltpu
from jax.sharding import PartitionSpec as P

MESH = pl.DeviceIdType.MESH
f32, bf16 = jnp.float32, jnp.bfloat16
ROWS, WIDTH, BLK = 1024, 256, 128
BC = ROWS // BLK
KL, KC = 6, 2
CH = 8
TR = 256
COMBOS = sorted(itertools.combinations(range(5), 3), key=lambda bits: sum(1 << b for b in bits))
TOTALS = [sum(1 << b for b in bits) for bits in COMBOS]


def flip(index, mask):
    bit, out = 1, index
    while bit <= mask:
        if mask & bit:
            out = out + bit * (1 - 2 * lax.rem(lax.div(index, bit), 2))
        bit *= 2
    return out


def dot(a, b):
    return jnp.dot(a, b, preferred_element_type=f32)


def split(x):
    hi = x.astype(bf16)
    return hi, (x - hi.astype(f32)).astype(bf16)


def rows_of(m, size):
    return pl.ds(pl.multiple_of(m * size, size), size)


def kernel(
    bits, local_cols, couple_cols, partners, bounds, v_hbm, local_hbm, couple_hbm, rot_hbm, out_hbm,
    own, mate, acc, other, own_blocks, turned, couple, outgoing, mate_blocks, h_local, h_couple,
    src_hi, src_lo, mate_hi, mate_lo, rot, rot_hi, rot_lo, part_hi, part_lo, out_v,
    in_sem, rot_sem, out_sem, send, recv, b_send, b_recv, g_send, g_recv,
):
    row, band = lax.axis_index("rows"), lax.axis_index("bands")
    relay = None
    for low, high in ((0, 1), (3, 4)):
        if low in bits and high in bits:
            relay = (1, 2)
            bits = tuple(b for b in bits if b not in (low, high)) + (low, high)
    masks = [1 << b for b in bits]
    direct = [p for p in range(3) if relay is None or p != relay[1]]
    shared = () if relay is None or 2 in bits else (1, 2)
    mates = [(flip(row, m), band) for m in masks]
    twin = (row, flip(band, 1))
    across = (row, flip(band, 2))
    peers = mates + [twin, across]
    if relay is not None:
        onward = (flip(row, masks[relay[0]] | masks[relay[1]]), band)
        peers.append(onward)

    def remote(src, dst, send_sem, recv_sem, to):
        return pltpu.make_async_remote_copy(
            src_ref=src, dst_ref=dst, send_sem=send_sem, recv_sem=recv_sem, device_id=to, device_id_type=MESH
        )

    loads = [
        pltpu.make_async_copy(couple_hbm, couple, in_sem.at[0]),
        pltpu.make_async_copy(local_hbm, own_blocks, in_sem.at[1]),
        pltpu.make_async_copy(v_hbm, own.at[0], in_sem.at[2]),
    ]
    for load in loads:
        load.start()
    rot_loads = []
    for g in range(4):
        piece = rot_hbm.at[rows_of(flip(band, g), WIDTH), rows_of(band, WIDTH)]
        rot_loads.append(pltpu.make_async_copy(piece, rot.at[pl.ds(g * WIDTH, WIDTH)], rot_sem.at[g]))
        rot_loads[-1].start()

    barrier = pltpu.get_barrier_semaphore()
    for peer in peers:
        pl.semaphore_signal(barrier, inc=1, device_id=peer, device_id_type=MESH)
    pl.semaphore_wait(barrier, len(peers))

    def chunk(ph, p, c, source=None):
        rs = rows_of(c, BLK)
        if p in direct:
            source, to = own.at[ph] if source is None else source, mates[p]
        else:
            source, to = mate.at[ph, relay[0]], onward
        return remote(source.at[rs], mate.at[ph, p, rs], send.at[ph, p, c], recv.at[ph, p, c], to)

    def pass_on(ph, c):
        if relay is not None:
            chunk(ph, relay[0], c).wait_recv()
            chunk(ph, relay[1], c).start()

    for p in direct:
        chunk(0, p, 0, v_hbm).start()

    colours = []
    for m in masks:
        colour = jnp.int32(0)
        for c in (1, 2):
            colour = colour + jnp.where(partners[c, 0] == m, c, 0)
        colours.append(colour)

    counts = [BC * KC // (4 if p in shared else 2) for p in range(3)]
    firsts = [counts[p] * (band if p in shared else lax.rem(band, 2)) for p in range(3)]
    loads[0].wait()
    blocks = []
    for p in range(3):
        count, first = counts[p], firsts[p]

        @pl.loop(0, count // 2)
        def _(q, p=p, first=first):
            for u in range(2):
                outgoing[p, q * 2 + u] = couple[colours[p], first + q * 2 + u]

        blocks.append(
            remote(
                outgoing.at[p, pl.ds(0, count)], mate_blocks.at[p, pl.ds(first, count)],
                b_send.at[0, p], b_recv.at[0, p], mates[p],
            )
        )
        blocks[-1].start()

    @pl.loop(1, CH)
    def _(c):
        for p in direct:
            chunk(0, p, c, v_hbm).start()

    def turn(source, number):
        @pl.loop(0, number // 4)
        def _(q):
            for u in range(4):
                turned[q * 4 + u] = source[q * 4 + u].T

    def one_if(flag):
        return jnp.where(flag, 1.0, 0.0).astype(f32)

    def added(terms):
        return functools.reduce(lambda a, b: a + b, terms)

    loads[1].wait()
    turn(own_blocks, BC * KL)

    @pl.loop(0, BC)
    def _(i):
        rs = rows_of(i, BLK)

        @pl.loop(0, BC // 2)
        def _(q):
            for u in range(2):
                j = q * 2 + u
                total = added(
                    [own_blocks[i * KL + k] * one_if(local_cols[i, k] == j) for k in range(KL)]
                    + [turned[j * KL + k] * one_if(local_cols[j, k] == i) for k in range(KL)]
                )
                hi, lo = split(total)
                h_local[rs, rows_of(j, BLK)] = hi
                h_local[rs, rows_of(BC + j, BLK)] = lo

    loads[2].wait()

    @pl.loop(0, ROWS // TR)
    def _(m):
        rs = rows_of(m, TR)
        src_hi[rs], src_lo[rs] = split(own[0, rs])

    def forward(kind, p, at, to):
        span = mate_blocks.at[p, pl.ds(at, counts[p])]
        return remote(span, span, b_send.at[kind, p], b_recv.at[kind, p], to)

    to_twin = [forward(1, p, firsts[p], twin) for p in range(3)]
    to_across = {p: forward(2, p, firsts[p], across) for p in shared}
    far_to_twin = {p: forward(3, p, counts[p] * flip(band, 2), twin) for p in shared}

    def build_couple():
        pass_on(0, 0)
        for p in (1, 2, 0):
            blocks[p].wait_recv()
            if p in shared:
                to_across[p].start()
            to_twin[p].start()

        @pl.loop(0, 3)
        def _(p):
            def pick(values):
                return jnp.where(p == 0, values[0], jnp.where(p == 1, values[1], values[2]))

            colour = pick(colours)
            here, there = row * BC, pick([m[0] for m in mates]) * BC

            for k in range(3):
                @pl.when(p == k)
                def _(k=k):
                    if k in shared:
                        to_across[k].wait_recv()
                        far_to_twin[k].start()
                    to_twin[k].wait_recv()
                    if k in shared:
                        far_to_twin[k].wait_recv()

            turn(mate_blocks.at[p], BC * KC)

            @pl.loop(0, BC)
            def _(i):
                rs = rows_of(i, BLK)

                @pl.loop(0, BC // 2)
                def _(q):
                    for u in range(2):
                        j = q * 2 + u
                        total = added(
                            [
                                couple[colour, i * KC + k] * one_if(couple_cols[colour, k, here + i] == j)
                                for k in range(KC)
                            ]
                            + [
                                turned[j * KC + k] * one_if(couple_cols[colour, k, there + j] == i)
                                for k in range(KC)
                            ]
                        )
                        hi, lo = split(total)
                        at = p * 2 + u
                        h_couple[q, rs, rows_of(at, BLK)] = hi
                        h_couple[q, rs, rows_of(6 + at, BLK)] = lo

            if relay is not None:
                pass_on(0, 1 + p + jnp.where(p == 2, 1, 0))

                @pl.when(p > 0)
                def _():
                    pass_on(0, 1 + 2 * p)

    def couple_product(kc, rs):
        return (
            dot(h_couple[kc, rs, :3 * TR], mate_hi[...])
            + dot(h_couple[kc, rs, 3 * TR:], mate_hi[...])
            + dot(h_couple[kc, rs, :3 * TR], mate_lo[...])
        )

    def receive(ph, kc):
        if relay is not None:
            @pl.when((ph == 1) & (kc == 0))
            def _():
                pass_on(1, 0)
                pass_on(1, 1)

            @pl.when((ph == 1) & (kc < 3))
            def _():
                pass_on(1, 2 * kc + 2)
                pass_on(1, 2 * kc + 3)

            @pl.when((ph == 0) & ((kc == 1) | (kc == 2)))
            def _():
                pass_on(0, kc + 5)

        for e in range(2):
            for p in range(3):
                if relay is None or p != relay[0]:
                    chunk(ph, p, 2 * kc + e).wait_recv()
        for p in range(3):
            hi, lo = split(mate[ph, p, rows_of(kc, TR)])
            mate_hi[p * TR:(p + 1) * TR] = hi
            mate_lo[p * TR:(p + 1) * TR] = lo

    wide = (1, WIDTH)
    lowest, lower, upper = (jnp.full(wide, bounds[i], f32) for i in range(3))
    half_width = (upper - lower) / 2.0
    centre = (upper + lower) / 2.0
    sigma_one = half_width / (lowest - centre)
    sigma_two = 1.0 / (2.0 / sigma_one - sigma_one)

    def hand(kind, m):
        rs = rows_of(m, TR)
        source = other.at[1] if kind == 2 else own.at[2]
        return remote(
            source.at[rs], other.at[kind, rs], g_send.at[kind, m], g_recv.at[kind, m], across if kind == 1 else twin
        )

    @pl.loop(0, 2)
    def _(ph):
        @pl.loop(0, ROWS // TR)
        def _(m):
            rs = rows_of(m, TR)
            acc[rs] = (
                dot(h_local[rs, :ROWS], src_hi[...])
                + dot(h_local[rs, ROWS:], src_hi[...])
                + dot(h_local[rs, :ROWS], src_lo[...])
            )

        @pl.when(ph == 0)
        def _():
            build_couple()

        @pl.loop(0, 3)
        def _(kc):
            receive(ph, kc)

            @pl.loop(0, ROWS // TR)
            def _(m):
                rs = rows_of(m, TR)
                acc[rs] += couple_product(kc, rs)

        receive(ph, jnp.int32(3))
        outer = jnp.where(ph == 0, sigma_one, 2.0 * sigma_two) / half_width
        back = jnp.where(ph == 0, 0.0, sigma_one * sigma_two)

        @pl.loop(0, ROWS // TR)
        def _(m):
            rs = rows_of(m, TR)
            total = acc[rs] + couple_product(3, rs)
            result = (total - centre * own[ph, rs]) * outer - back * own[0, rs]
            own[ph + 1, rs] = result

            @pl.when(ph == 0)
            def _():
                for e in range(2):
                    for p in direct:
                        chunk(1, p, 2 * m + e).start()

            @pl.when(ph == 1)
            def _():
                hand(1, m).start()
                hand(0, m).start()

            src_hi[rs], src_lo[rs] = split(result)

    for load in rot_loads:
        load.wait()

    @pl.loop(0, 4)
    def _(g):
        rs = rows_of(g, WIDTH)
        rot_hi[rs], rot_lo[rs] = split(rot[rs])

    def store(m):
        rs = rows_of(m, TR)
        return pltpu.make_async_copy(out_v.at[rs], out_hbm.at[rs], out_sem.at[m])

    @pl.loop(0, ROWS // TR)
    def _(m):
        rs = rows_of(m, TR)
        hand(1, m).wait_recv()
        hand(2, m).start()
        hand(0, m).wait_recv()
        part_hi[:, :WIDTH] = src_hi[rs]
        part_lo[:, :WIDTH] = src_lo[rs]
        for g in (1, 2):
            gs = slice(g * WIDTH, (g + 1) * WIDTH)
            part_hi[:, gs], part_lo[:, gs] = split(other[g - 1, rs])
        gs = slice(0, 3 * WIDTH)
        total = dot(part_hi[:, gs], rot_hi[gs]) + dot(part_lo[:, gs], rot_hi[gs]) + dot(part_hi[:, gs], rot_lo[gs])
        hand(2, m).wait_recv()
        hi, lo = split(other[2, rs])
        gs = slice(3 * WIDTH, 4 * WIDTH)
        out_v[rs] = total + (dot(hi, rot_hi[gs]) + dot(lo, rot_hi[gs]) + dot(hi, rot_lo[gs]))
        store(m).start()

    @pl.loop(0, CH)
    def _(c):
        for ph in range(2):
            for p in range(3):
                chunk(ph, p, c).wait_send()

    for copy in blocks + to_twin + list(to_across.values()) + list(far_to_twin.values()):
        copy.wait_send()

    @pl.loop(0, ROWS // TR)
    def _(m):
        for kind in range(3):
            hand(kind, m).wait_send()
        store(m).wait()


def fused(bits, number):
    dma = pltpu.SemaphoreType.DMA
    scratch = [
        pltpu.VMEM((3, ROWS, WIDTH), f32),
        pltpu.VMEM((2, 3, ROWS, WIDTH), f32),
        pltpu.VMEM((ROWS, WIDTH), f32),
        pltpu.VMEM((3, ROWS, WIDTH), f32),
        pltpu.VMEM((BC * KL, BLK, BLK), f32),
        pltpu.VMEM((BC * KL, BLK, BLK), f32),
        pltpu.VMEM((3, BC * KC, BLK, BLK), f32),
        pltpu.VMEM((3, BC * KC // 2, BLK, BLK), f32),
        pltpu.VMEM((3, BC * KC, BLK, BLK), f32),
        pltpu.VMEM((ROWS, 2 * ROWS), bf16),
        pltpu.VMEM((4, ROWS, 6 * TR), bf16),
        pltpu.VMEM((ROWS, WIDTH), bf16),
        pltpu.VMEM((ROWS, WIDTH), bf16),
        pltpu.VMEM((3 * TR, WIDTH), bf16),
        pltpu.VMEM((3 * TR, WIDTH), bf16),
        pltpu.VMEM((4 * WIDTH, WIDTH), f32),
        pltpu.VMEM((4 * WIDTH, WIDTH), bf16),
        pltpu.VMEM((4 * WIDTH, WIDTH), bf16),
        pltpu.VMEM((TR, 4 * WIDTH), bf16),
        pltpu.VMEM((TR, 4 * WIDTH), bf16),
        pltpu.VMEM((ROWS, WIDTH), f32),
        dma((3,)), dma((4,)), dma((4,)),
        dma((2, 3, CH)), dma((2, 3, CH)),
        dma((4, 3)), dma((4, 3)),
        dma((3, 4)), dma((3, 4)),
    ]
    smem, hbm = pl.BlockSpec(memory_space=pltpu.SMEM), pl.BlockSpec(memory_space=pl.ANY)
    return pl.pallas_call(
        functools.partial(kernel, bits),
        out_shape=jax.ShapeDtypeStruct((ROWS, WIDTH), f32),
        in_specs=[smem] * 4 + [hbm] * 4,
        out_specs=hbm,
        scratch_shapes=scratch,
        compiler_params=pltpu.CompilerParams(
            collective_id=number, has_side_effects=True, vmem_limit_bytes=60 << 20
        ),
        name="filter_" + "".join(map(str, bits)),
    )


def local(
    vectors, local_blocks, local_cols, coupling_blocks, coupling_cols, partners, bounds, rotation
):
    total = partners[0, 0] + partners[1, 0] + partners[2, 0]
    index = sum((total > t).astype(jnp.int32) for t in TOTALS[:-1])
    return lax.switch(
        index,
        [fused(bits, number) for number, bits in enumerate(COMBOS)],
        local_cols, coupling_cols.transpose(0, 2, 1), partners, bounds, vectors,
        local_blocks.reshape(BC * KL, BLK, BLK),
        coupling_blocks.reshape(3, BC * KC, BLK, BLK),
        rotation,
    )


def solution(mesh):
    in_specs = (
        P("rows", "bands"),
        P("rows", None, None, None),
        P("rows", None),
        P(None, "rows", None, None, None),
        P(),
        P(),
        P(),
        P(),
    )
    out_specs = P("rows", "bands")
    return jax.shard_map(local, mesh=mesh, in_specs=in_specs, out_specs=out_specs, check_vma=False)
```

```python
import functools
import itertools

import jax
import jax.numpy as jnp
from jax import lax
from jax.experimental import pallas as pl
from jax.experimental.pallas import tpu as pltpu
from jax.sharding import PartitionSpec as P

MESH = pl.DeviceIdType.MESH
f32, bf16 = jnp.float32, jnp.bfloat16
ROWS, WIDTH, BLK = 1024, 256, 128
BC = ROWS // BLK
KL, KC = 6, 2
CH = 8
TR = 256
COMBOS = sorted(itertools.combinations(range(5), 3), key=lambda bits: sum(1 << b for b in bits))
TOTALS = [sum(1 << b for b in bits) for bits in COMBOS]


def flip(index, mask):
    bit, out = 1, index
    while bit <= mask:
        if mask & bit:
            out = out + bit * (1 - 2 * lax.rem(lax.div(index, bit), 2))
        bit *= 2
    return out


def dot(a, b):
    return jnp.dot(a, b, preferred_element_type=f32)


def split(x):
    hi = x.astype(bf16)
    return hi, (x - hi.astype(f32)).astype(bf16)


def rows_of(m, size):
    return pl.ds(pl.multiple_of(m * size, size), size)


def kernel(
    bits, local_cols, couple_cols, partners, bounds, v_hbm, local_hbm, couple_hbm, rot_hbm, out_hbm,
    v_own, own, mate, acc, other, own_blocks, turned, couple, outgoing, mate_blocks, h_local, h_couple,
    src_hi, src_lo, mate_hi, mate_lo, rot, rot_hi, rot_lo, part_hi, part_lo, out_v,
    in_sem, rot_sem, out_sem, send, recv, b_send, b_recv, g_send, g_recv,
):
    row, band = lax.axis_index("rows"), lax.axis_index("bands")
    relay = None
    for low, high in ((0, 1), (3, 4)):
        if low in bits and high in bits:
            relay = (1, 2)
            bits = tuple(b for b in bits if b not in (low, high)) + (low, high)
    masks = [1 << b for b in bits]
    direct = [p for p in range(3) if relay is None or p != relay[1]]
    shared = () if relay is None or 2 in bits else (1, 2)
    mates = [(flip(row, m), band) for m in masks]
    twin = (row, flip(band, 1))
    across = (row, flip(band, 2))
    peers = mates + [twin, across]
    if relay is not None:
        onward = (flip(row, masks[relay[0]] | masks[relay[1]]), band)
        peers.append(onward)

    def remote(src, dst, send_sem, recv_sem, to):
        return pltpu.make_async_remote_copy(
            src_ref=src, dst_ref=dst, send_sem=send_sem, recv_sem=recv_sem, device_id=to, device_id_type=MESH
        )

    loads = [
        pltpu.make_async_copy(couple_hbm, couple, in_sem.at[0]),
        pltpu.make_async_copy(local_hbm, own_blocks, in_sem.at[1]),
        pltpu.make_async_copy(v_hbm, v_own, in_sem.at[2]),
    ]
    for load in loads:
        load.start()
    rot_loads = []
    for g in range(4):
        piece = rot_hbm.at[rows_of(flip(band, g), WIDTH), rows_of(band, WIDTH)]
        rot_loads.append(pltpu.make_async_copy(piece, rot.at[pl.ds(g * WIDTH, WIDTH)], rot_sem.at[g]))
        rot_loads[-1].start()

    barrier = pltpu.get_barrier_semaphore()
    for peer in peers:
        pl.semaphore_signal(barrier, inc=1, device_id=peer, device_id_type=MESH)
    pl.semaphore_wait(barrier, len(peers))

    def chunk(ph, p, c):
        rs = rows_of(c, BLK)
        if p in direct:
            source, to = own.at[ph], mates[p]
        else:
            source, to = mate.at[ph, relay[0]], onward
        return remote(source.at[rs], mate.at[ph, p, rs], send.at[ph, p, c], recv.at[ph, p, c], to)

    def pass_on(ph, c):
        if relay is not None:
            chunk(ph, relay[0], c).wait_recv()
            chunk(ph, relay[1], c).start()

    def hand(kind, m):
        rs = rows_of(m, TR)
        source = other.at[1] if kind == 2 else v_hbm
        return remote(
            source.at[rs], other.at[kind, rs], g_send.at[kind, m], g_recv.at[kind, m], across if kind == 1 else twin
        )

    hand(1, 0).start()
    hand(0, 0).start()

    colours = []
    for m in masks:
        colour = jnp.int32(0)
        for c in (1, 2):
            colour = colour + jnp.where(partners[c, 0] == m, c, 0)
        colours.append(colour)

    counts = [BC * KC // (4 if p in shared else 2) for p in range(3)]
    firsts = [counts[p] * (band if p in shared else lax.rem(band, 2)) for p in range(3)]
    loads[0].wait()
    blocks = []
    for p in range(3):
        count, first = counts[p], firsts[p]

        @pl.loop(0, count // 2)
        def _(q, p=p, first=first):
            for u in range(2):
                outgoing[p, q * 2 + u] = couple[colours[p], first + q * 2 + u]

        blocks.append(
            remote(
                outgoing.at[p, pl.ds(0, count)], mate_blocks.at[p, pl.ds(first, count)],
                b_send.at[0, p], b_recv.at[0, p], mates[p],
            )
        )
        blocks[-1].start()

    @pl.loop(1, ROWS // TR)
    def _(m):
        hand(1, m).start()
        hand(0, m).start()

    def turn(source, number):
        @pl.loop(0, number // 4)
        def _(q):
            for u in range(4):
                turned[q * 4 + u] = source[q * 4 + u].T

    def one_if(flag):
        return jnp.where(flag, 1.0, 0.0).astype(f32)

    def added(terms):
        return functools.reduce(lambda a, b: a + b, terms)

    def build_local():
        @pl.loop(0, BC)
        def _(i):
            rs = rows_of(i, BLK)

            @pl.loop(0, BC // 2)
            def _(q):
                for u in range(2):
                    j = q * 2 + u
                    total = added(
                        [own_blocks[i * KL + k] * one_if(local_cols[i, k] == j) for k in range(KL)]
                        + [turned[j * KL + k] * one_if(local_cols[j, k] == i) for k in range(KL)]
                    )
                    hi, lo = split(total)
                    h_local[rs, rows_of(j, BLK)] = hi
                    h_local[rs, rows_of(BC + j, BLK)] = lo

    def rotate(m):
        rs = rows_of(m, TR)
        hand(1, m).wait_recv()
        hand(2, m).start()
        hand(0, m).wait_recv()
        part_hi[:, :WIDTH], part_lo[:, :WIDTH] = split(v_own[rs])
        for g in (1, 2, 3):
            if g == 3:
                hand(2, m).wait_recv()
            gs = slice(g * WIDTH, (g + 1) * WIDTH)
            part_hi[:, gs], part_lo[:, gs] = split(other[g - 1, rs])
        turned_bands = (
            dot(part_hi[...], rot_hi[...]) + dot(part_lo[...], rot_hi[...]) + dot(part_hi[...], rot_lo[...])
        )
        own[0, rs] = turned_bands
        for e in range(2):
            for p in direct:
                chunk(0, p, 2 * m + e).start()
        src_hi[rs], src_lo[rs] = split(turned_bands)

    def forward(kind, p, at, to):
        span = mate_blocks.at[p, pl.ds(at, counts[p])]
        return remote(span, span, b_send.at[kind, p], b_recv.at[kind, p], to)

    to_twin = [forward(1, p, firsts[p], twin) for p in range(3)]
    to_across = {p: forward(2, p, firsts[p], across) for p in shared}
    far_to_twin = {p: forward(3, p, counts[p] * flip(band, 2), twin) for p in shared}

    for load in rot_loads:
        load.wait()

    @pl.loop(0, 4)
    def _(g):
        rs = rows_of(g, WIDTH)
        rot_hi[rs], rot_lo[rs] = split(rot[rs])

    loads[1].wait()
    loads[2].wait()

    def build_couple(p):
        def pick(values):
            return jnp.where(p == 0, values[0], jnp.where(p == 1, values[1], values[2]))

        colour = pick(colours)
        here, there = row * BC, pick([m[0] for m in mates]) * BC

        for k in range(3):
            @pl.when(p == k)
            def _(k=k):
                if k in shared:
                    to_across[k].wait_recv()
                    far_to_twin[k].start()
                to_twin[k].wait_recv()
                if k in shared:
                    far_to_twin[k].wait_recv()

        turn(mate_blocks.at[p], BC * KC)

        @pl.loop(0, BC)
        def _(i):
            rs = rows_of(i, BLK)

            @pl.loop(0, BC // 2)
            def _(q):
                for u in range(2):
                    j = q * 2 + u
                    total = added(
                        [
                            couple[colour, i * KC + k] * one_if(couple_cols[colour, k, here + i] == j)
                            for k in range(KC)
                        ]
                        + [
                            turned[j * KC + k] * one_if(couple_cols[colour, k, there + j] == i)
                            for k in range(KC)
                        ]
                    )
                    hi, lo = split(total)
                    at = p * 2 + u
                    h_couple[q, rs, rows_of(at, BLK)] = hi
                    h_couple[q, rs, rows_of(6 + at, BLK)] = lo

        if relay is not None:
            pass_on(0, 2 * p)
            pass_on(0, 2 * p + 1)

    @pl.loop(0, 5)
    def _(step):
        @pl.when(step == 0)
        def _():
            turn(own_blocks, BC * KL)

        @pl.when(step == 1)
        def _():
            build_local()
            for p in (1, 2, 0):
                blocks[p].wait_recv()
                if p in shared:
                    to_across[p].start()
                to_twin[p].start()

        @pl.when(step >= 2)
        def _():
            build_couple(step - 2)

        @pl.when(step < 4)
        def _():
            rotate(step)

    def couple_product(kc, rs):
        return (
            dot(h_couple[kc, rs, :3 * TR], mate_hi[...])
            + dot(h_couple[kc, rs, 3 * TR:], mate_hi[...])
            + dot(h_couple[kc, rs, :3 * TR], mate_lo[...])
        )

    def receive(ph, kc):
        if relay is not None:
            @pl.when((ph == 1) & (kc == 0))
            def _():
                pass_on(1, 0)
                pass_on(1, 1)

            @pl.when((ph == 1) & (kc < 3))
            def _():
                pass_on(1, 2 * kc + 2)
                pass_on(1, 2 * kc + 3)

            @pl.when((ph == 0) & ((kc == 1) | (kc == 2)))
            def _():
                pass_on(0, kc + 5)

        for e in range(2):
            for p in range(3):
                if relay is None or p != relay[0]:
                    chunk(ph, p, 2 * kc + e).wait_recv()
        for p in range(3):
            hi, lo = split(mate[ph, p, rows_of(kc, TR)])
            mate_hi[p * TR:(p + 1) * TR] = hi
            mate_lo[p * TR:(p + 1) * TR] = lo

    wide = (1, WIDTH)
    lowest, lower, upper = (jnp.full(wide, bounds[i], f32) for i in range(3))
    half_width = (upper - lower) / 2.0
    centre = (upper + lower) / 2.0
    sigma_one = half_width / (lowest - centre)
    sigma_two = 1.0 / (2.0 / sigma_one - sigma_one)

    def store(m):
        rs = rows_of(m, TR)
        return pltpu.make_async_copy(out_v.at[rs], out_hbm.at[rs], out_sem.at[m])

    @pl.loop(0, 2)
    def _(ph):
        @pl.loop(0, ROWS // TR)
        def _(m):
            rs = rows_of(m, TR)
            acc[rs] = (
                dot(h_local[rs, :ROWS], src_hi[...])
                + dot(h_local[rs, ROWS:], src_hi[...])
                + dot(h_local[rs, :ROWS], src_lo[...])
            )

        @pl.loop(0, 3)
        def _(kc):
            receive(ph, kc)

            @pl.loop(0, ROWS // TR)
            def _(m):
                rs = rows_of(m, TR)
                acc[rs] += couple_product(kc, rs)

        receive(ph, jnp.int32(3))
        outer = jnp.where(ph == 0, sigma_one, 2.0 * sigma_two) / half_width
        back = jnp.where(ph == 0, 0.0, sigma_one * sigma_two)

        @pl.loop(0, ROWS // TR)
        def _(m):
            rs = rows_of(m, TR)
            total = acc[rs] + couple_product(3, rs)
            result = (total - centre * own[ph, rs]) * outer - back * own[0, rs]

            @pl.when(ph == 0)
            def _():
                own[1, rs] = result
                for e in range(2):
                    for p in direct:
                        chunk(1, p, 2 * m + e).start()
                src_hi[rs], src_lo[rs] = split(result)

            @pl.when(ph == 1)
            def _():
                out_v[rs] = result
                store(m).start()

    @pl.loop(0, CH)
    def _(c):
        for ph in range(2):
            for p in range(3):
                chunk(ph, p, c).wait_send()

    for copy in blocks + to_twin + list(to_across.values()) + list(far_to_twin.values()):
        copy.wait_send()

    @pl.loop(0, ROWS // TR)
    def _(m):
        for kind in range(3):
            hand(kind, m).wait_send()
        store(m).wait()


def fused(bits, number):
    dma = pltpu.SemaphoreType.DMA
    scratch = [
        pltpu.VMEM((ROWS, WIDTH), f32),
        pltpu.VMEM((2, ROWS, WIDTH), f32),
        pltpu.VMEM((2, 3, ROWS, WIDTH), f32),
        pltpu.VMEM((ROWS, WIDTH), f32),
        pltpu.VMEM((3, ROWS, WIDTH), f32),
        pltpu.VMEM((BC * KL, BLK, BLK), f32),
        pltpu.VMEM((BC * KL, BLK, BLK), f32),
        pltpu.VMEM((3, BC * KC, BLK, BLK), f32),
        pltpu.VMEM((3, BC * KC // 2, BLK, BLK), f32),
        pltpu.VMEM((3, BC * KC, BLK, BLK), f32),
        pltpu.VMEM((ROWS, 2 * ROWS), bf16),
        pltpu.VMEM((4, ROWS, 6 * TR), bf16),
        pltpu.VMEM((ROWS, WIDTH), bf16),
        pltpu.VMEM((ROWS, WIDTH), bf16),
        pltpu.VMEM((3 * TR, WIDTH), bf16),
        pltpu.VMEM((3 * TR, WIDTH), bf16),
        pltpu.VMEM((4 * WIDTH, WIDTH), f32),
        pltpu.VMEM((4 * WIDTH, WIDTH), bf16),
        pltpu.VMEM((4 * WIDTH, WIDTH), bf16),
        pltpu.VMEM((TR, 4 * WIDTH), bf16),
        pltpu.VMEM((TR, 4 * WIDTH), bf16),
        pltpu.VMEM((ROWS, WIDTH), f32),
        dma((3,)), dma((4,)), dma((4,)),
        dma((2, 3, CH)), dma((2, 3, CH)),
        dma((4, 3)), dma((4, 3)),
        dma((3, 4)), dma((3, 4)),
    ]
    smem, hbm = pl.BlockSpec(memory_space=pltpu.SMEM), pl.BlockSpec(memory_space=pl.ANY)
    return pl.pallas_call(
        functools.partial(kernel, bits),
        out_shape=jax.ShapeDtypeStruct((ROWS, WIDTH), f32),
        in_specs=[smem] * 4 + [hbm] * 4,
        out_specs=hbm,
        scratch_shapes=scratch,
        compiler_params=pltpu.CompilerParams(
            collective_id=number, has_side_effects=True, vmem_limit_bytes=60 << 20
        ),
        name="filter_" + "".join(map(str, bits)),
    )


def local(
    vectors, local_blocks, local_cols, coupling_blocks, coupling_cols, partners, bounds, rotation
):
    total = partners[0, 0] + partners[1, 0] + partners[2, 0]
    index = sum((total > t).astype(jnp.int32) for t in TOTALS[:-1])
    return lax.switch(
        index,
        [fused(bits, number) for number, bits in enumerate(COMBOS)],
        local_cols, coupling_cols.transpose(0, 2, 1), partners, bounds, vectors,
        local_blocks.reshape(BC * KL, BLK, BLK),
        coupling_blocks.reshape(3, BC * KC, BLK, BLK),
        rotation,
    )


def solution(mesh):
    in_specs = (
        P("rows", "bands"),
        P("rows", None, None, None),
        P("rows", None),
        P(None, "rows", None, None, None),
        P(),
        P(),
        P(),
        P(),
    )
    out_specs = P("rows", "bands")
    return jax.shard_map(local, mesh=mesh, in_specs=in_specs, out_specs=out_specs, check_vma=False)
```

```python
import functools
import itertools

import jax
import jax.numpy as jnp
from jax import lax
from jax.experimental import pallas as pl
from jax.experimental.pallas import tpu as pltpu
from jax.sharding import PartitionSpec as P

MESH = pl.DeviceIdType.MESH
f32, bf16 = jnp.float32, jnp.bfloat16
ROWS, WIDTH, BLK = 1024, 256, 128
BC = ROWS // BLK
KL, KC = 6, 2
CH = 8
TR = 256
COMBOS = sorted(itertools.combinations(range(5), 3), key=lambda bits: sum(1 << b for b in bits))
TOTALS = [sum(1 << b for b in bits) for bits in COMBOS]


def flip(index, mask):
    bit, out = 1, index
    while bit <= mask:
        if mask & bit:
            out = out + bit * (1 - 2 * lax.rem(lax.div(index, bit), 2))
        bit *= 2
    return out


def dot(a, b):
    return jnp.dot(a, b, preferred_element_type=f32)


def split(x):
    hi = x.astype(bf16)
    return hi, (x - hi.astype(f32)).astype(bf16)


def rows_of(m, size):
    return pl.ds(pl.multiple_of(m * size, size), size)


def kernel(
    bits, local_cols, couple_cols, partners, bounds, v_hbm, local_hbm, couple_hbm, rot_hbm, out_hbm,
    v_own, own, mate, acc, other, own_blocks, turned, couple, outgoing, mate_blocks, h_local, h_couple,
    src_hi, src_lo, mate_hi, mate_lo, rot, rot_hi, rot_lo, part_hi, part_lo, out_v,
    in_sem, rot_sem, out_sem, send, recv, b_send, b_recv, g_send, g_recv,
):
    row, band = lax.axis_index("rows"), lax.axis_index("bands")
    relay = None
    for low, high in ((0, 1), (3, 4)):
        if low in bits and high in bits:
            relay = (1, 2)
            bits = tuple(b for b in bits if b not in (low, high)) + (low, high)
    masks = [1 << b for b in bits]
    direct = [p for p in range(3) if relay is None or p != relay[1]]
    beside = bits.index(2) if 2 in bits else None
    shared = (beside,) if beside is not None else (2,)
    mates = [(flip(row, m), band) for m in masks]
    twin = (row, flip(band, 1))
    across = (row, flip(band, 2))
    peers = mates + [twin, across]
    if beside is not None:
        aslant = (flip(row, 4), flip(band, 2))
        peers.append(aslant)
    if relay is not None:
        onward = (flip(row, masks[relay[0]] | masks[relay[1]]), band)
        peers.append(onward)

    def remote(src, dst, send_sem, recv_sem, to):
        return pltpu.make_async_remote_copy(
            src_ref=src, dst_ref=dst, send_sem=send_sem, recv_sem=recv_sem, device_id=to, device_id_type=MESH
        )

    loads = [
        pltpu.make_async_copy(couple_hbm, couple, in_sem.at[0]),
        pltpu.make_async_copy(local_hbm, own_blocks, in_sem.at[1]),
        pltpu.make_async_copy(v_hbm, v_own, in_sem.at[2]),
    ]
    for load in loads:
        load.start()
    rot_loads = []
    for g in range(4):
        piece = rot_hbm.at[rows_of(flip(band, g), WIDTH), rows_of(band, WIDTH)]
        rot_loads.append(pltpu.make_async_copy(piece, rot.at[pl.ds(g * WIDTH, WIDTH)], rot_sem.at[g]))
        rot_loads[-1].start()

    barrier = pltpu.get_barrier_semaphore()
    for peer in peers:
        pl.semaphore_signal(barrier, inc=1, device_id=peer, device_id_type=MESH)
    pl.semaphore_wait(barrier, len(peers))

    def chunk(ph, p, c):
        rs = rows_of(c, BLK)
        if p in direct:
            source, to = own.at[ph], mates[p]
        else:
            source, to = mate.at[ph, relay[0]], onward
        return remote(source.at[rs], mate.at[ph, p, rs], send.at[ph, p, c], recv.at[ph, p, c], to)

    def pass_on(ph, c):
        if relay is not None:
            chunk(ph, relay[0], c).wait_recv()
            chunk(ph, relay[1], c).start()

    def hand(kind, m):
        rs = rows_of(m, TR)
        source = other.at[1] if kind == 2 else v_hbm
        return remote(
            source.at[rs], other.at[kind, rs], g_send.at[kind, m], g_recv.at[kind, m], across if kind == 1 else twin
        )

    hand(1, 0).start()
    hand(0, 0).start()

    colours = []
    for m in masks:
        colour = jnp.int32(0)
        for c in (1, 2):
            colour = colour + jnp.where(partners[c, 0] == m, c, 0)
        colours.append(colour)

    counts = [BC * KC // (4 if p in shared else 2) for p in range(3)]
    firsts = [counts[p] * (band if p in shared else lax.rem(band, 2)) for p in range(3)]
    loads[0].wait()
    blocks = []
    for p in range(3):
        count, first = counts[p], firsts[p]

        @pl.loop(0, count // 2)
        def _(q, p=p, first=first):
            for u in range(2):
                outgoing[p, q * 2 + u] = couple[colours[p], first + q * 2 + u]

        blocks.append(
            remote(
                outgoing.at[p, pl.ds(0, count)], mate_blocks.at[p, pl.ds(first, count)],
                b_send.at[0, p], b_recv.at[0, p], mates[p],
            )
        )
        blocks[-1].start()
        if p == beside:
            to_aslant = remote(
                outgoing.at[p, pl.ds(0, count)], mate_blocks.at[p, pl.ds(first, count)],
                b_send.at[2, p], b_recv.at[2, p], aslant,
            )
            to_aslant.start()

    @pl.loop(1, ROWS // TR - (1 if beside is None else 0))
    def _(m):
        hand(1, m).start()
        hand(0, m).start()

    def turn(source, number):
        @pl.loop(0, number // 4)
        def _(q):
            for u in range(4):
                turned[q * 4 + u] = source[q * 4 + u].T

    def one_if(flag):
        return jnp.where(flag, 1.0, 0.0).astype(f32)

    def added(terms):
        return functools.reduce(lambda a, b: a + b, terms)

    def build_local():
        @pl.loop(0, BC)
        def _(i):
            rs = rows_of(i, BLK)

            @pl.loop(0, BC // 2)
            def _(q):
                for u in range(2):
                    j = q * 2 + u
                    total = added(
                        [own_blocks[i * KL + k] * one_if(local_cols[i, k] == j) for k in range(KL)]
                        + [turned[j * KL + k] * one_if(local_cols[j, k] == i) for k in range(KL)]
                    )
                    hi, lo = split(total)
                    h_local[rs, rows_of(j, BLK)] = hi
                    h_local[rs, rows_of(BC + j, BLK)] = lo

    def rotate(m):
        rs = rows_of(m, TR)
        hand(1, m).wait_recv()
        hand(2, m).start()
        hand(0, m).wait_recv()
        part_hi[:, :WIDTH], part_lo[:, :WIDTH] = split(v_own[rs])
        for g in (1, 2, 3):
            if g == 3:
                hand(2, m).wait_recv()
            gs = slice(g * WIDTH, (g + 1) * WIDTH)
            part_hi[:, gs], part_lo[:, gs] = split(other[g - 1, rs])
        turned_bands = (
            dot(part_hi[...], rot_hi[...]) + dot(part_lo[...], rot_hi[...]) + dot(part_hi[...], rot_lo[...])
        )
        own[0, rs] = turned_bands
        for e in range(2):
            for p in direct:
                chunk(0, p, 2 * m + e).start()
        src_hi[rs], src_lo[rs] = split(turned_bands)

    def forward(kind, p, at, to):
        span = mate_blocks.at[p, pl.ds(at, counts[p])]
        return remote(span, span, b_send.at[kind, p], b_recv.at[kind, p], to)

    to_twin = [forward(1, p, firsts[p], twin) for p in range(3)]
    to_across = {p: to_aslant if p == beside else forward(2, p, firsts[p], across) for p in shared}
    far_to_twin = {p: forward(3, p, counts[p] * flip(band, 2), twin) for p in shared}

    for load in rot_loads:
        load.wait()

    @pl.loop(0, 4)
    def _(g):
        rs = rows_of(g, WIDTH)
        rot_hi[rs], rot_lo[rs] = split(rot[rs])

    loads[1].wait()
    loads[2].wait()

    def build_couple(p):
        def pick(values):
            return jnp.where(p == 0, values[0], jnp.where(p == 1, values[1], values[2]))

        colour = pick(colours)
        here, there = row * BC, pick([m[0] for m in mates]) * BC

        for k in range(3):
            @pl.when(p == k)
            def _(k=k):
                if k in shared:
                    to_across[k].wait_recv()
                    far_to_twin[k].start()
                to_twin[k].wait_recv()
                if k in shared:
                    far_to_twin[k].wait_recv()

        turn(mate_blocks.at[p], BC * KC)

        @pl.loop(0, BC)
        def _(i):
            rs = rows_of(i, BLK)

            @pl.loop(0, BC // 2)
            def _(q):
                for u in range(2):
                    j = q * 2 + u
                    total = added(
                        [
                            couple[colour, i * KC + k] * one_if(couple_cols[colour, k, here + i] == j)
                            for k in range(KC)
                        ]
                        + [
                            turned[j * KC + k] * one_if(couple_cols[colour, k, there + j] == i)
                            for k in range(KC)
                        ]
                    )
                    hi, lo = split(total)
                    at = p * 2 + u
                    h_couple[q, rs, rows_of(at, BLK)] = hi
                    h_couple[q, rs, rows_of(6 + at, BLK)] = lo

        if relay is not None:
            @pl.when(p < 2)
            def _():
                pass_on(0, p)

            @pl.when(p == 1)
            def _():
                pass_on(0, 2)

    @pl.loop(0, 5)
    def _(step):
        @pl.when(step == 0)
        def _():
            turn(own_blocks, BC * KL)

        @pl.when(step == 1)
        def _():
            build_local()
            for p in (1, 2, 0):
                blocks[p].wait_recv()
                if p in shared and p != beside:
                    to_across[p].start()
                to_twin[p].start()
            if beside is None:
                hand(1, 3).start()
                hand(0, 3).start()

        @pl.when(step >= 2)
        def _():
            build_couple(step - 2)

        @pl.when(step != 3)
        def _():
            rotate(step - jnp.where(step == 4, 1, 0))

    pass_on(0, 3)
    pass_on(0, 4)

    def couple_product(kc, rs):
        return (
            dot(h_couple[kc, rs, :3 * TR], mate_hi[...])
            + dot(h_couple[kc, rs, 3 * TR:], mate_hi[...])
            + dot(h_couple[kc, rs, :3 * TR], mate_lo[...])
        )

    def receive(ph, kc):
        if relay is not None:
            @pl.when((ph == 1) & (kc == 0))
            def _():
                pass_on(1, 0)
                pass_on(1, 1)

            @pl.when((ph == 1) & (kc < 3))
            def _():
                pass_on(1, 2 * kc + 2)
                pass_on(1, 2 * kc + 3)

            @pl.when((ph == 0) & (kc < 2))
            def _():
                pass_on(0, kc + 5)

            @pl.when((ph == 0) & (kc == 1))
            def _():
                pass_on(0, 7)

        for e in range(2):
            for p in range(3):
                if relay is None or p != relay[0]:
                    chunk(ph, p, 2 * kc + e).wait_recv()
        for p in range(3):
            hi, lo = split(mate[ph, p, rows_of(kc, TR)])
            mate_hi[p * TR:(p + 1) * TR] = hi
            mate_lo[p * TR:(p + 1) * TR] = lo

    wide = (1, WIDTH)
    lowest, lower, upper = (jnp.full(wide, bounds[i], f32) for i in range(3))
    half_width = (upper - lower) / 2.0
    centre = (upper + lower) / 2.0
    sigma_one = half_width / (lowest - centre)
    sigma_two = 1.0 / (2.0 / sigma_one - sigma_one)

    def store(m):
        rs = rows_of(m, TR)
        return pltpu.make_async_copy(out_v.at[rs], out_hbm.at[rs], out_sem.at[m])

    @pl.loop(0, 2)
    def _(ph):
        @pl.loop(0, ROWS // TR)
        def _(m):
            rs = rows_of(m, TR)
            acc[rs] = (
                dot(h_local[rs, :ROWS], src_hi[...])
                + dot(h_local[rs, ROWS:], src_hi[...])
                + dot(h_local[rs, :ROWS], src_lo[...])
            )

        @pl.loop(0, 3)
        def _(kc):
            receive(ph, kc)

            @pl.loop(0, ROWS // TR)
            def _(m):
                rs = rows_of(m, TR)
                acc[rs] += couple_product(kc, rs)

        receive(ph, jnp.int32(3))
        outer = jnp.where(ph == 0, sigma_one, 2.0 * sigma_two) / half_width
        back = jnp.where(ph == 0, 0.0, sigma_one * sigma_two)

        @pl.loop(0, ROWS // TR)
        def _(m):
            rs = rows_of(m, TR)
            total = acc[rs] + couple_product(3, rs)
            result = (total - centre * own[ph, rs]) * outer - back * own[0, rs]

            @pl.when(ph == 0)
            def _():
                own[1, rs] = result
                for e in range(2):
                    for p in direct:
                        chunk(1, p, 2 * m + e).start()
                src_hi[rs], src_lo[rs] = split(result)

            @pl.when(ph == 1)
            def _():
                out_v[rs] = result
                store(m).start()

    @pl.loop(0, CH)
    def _(c):
        for ph in range(2):
            for p in range(3):
                chunk(ph, p, c).wait_send()

    for copy in blocks + to_twin + list(to_across.values()) + list(far_to_twin.values()):
        copy.wait_send()

    @pl.loop(0, ROWS // TR)
    def _(m):
        for kind in range(3):
            hand(kind, m).wait_send()
        store(m).wait()


def fused(bits, number):
    dma = pltpu.SemaphoreType.DMA
    scratch = [
        pltpu.VMEM((ROWS, WIDTH), f32),
        pltpu.VMEM((2, ROWS, WIDTH), f32),
        pltpu.VMEM((2, 3, ROWS, WIDTH), f32),
        pltpu.VMEM((ROWS, WIDTH), f32),
        pltpu.VMEM((3, ROWS, WIDTH), f32),
        pltpu.VMEM((BC * KL, BLK, BLK), f32),
        pltpu.VMEM((BC * KL, BLK, BLK), f32),
        pltpu.VMEM((3, BC * KC, BLK, BLK), f32),
        pltpu.VMEM((3, BC * KC // 2, BLK, BLK), f32),
        pltpu.VMEM((3, BC * KC, BLK, BLK), f32),
        pltpu.VMEM((ROWS, 2 * ROWS), bf16),
        pltpu.VMEM((4, ROWS, 6 * TR), bf16),
        pltpu.VMEM((ROWS, WIDTH), bf16),
        pltpu.VMEM((ROWS, WIDTH), bf16),
        pltpu.VMEM((3 * TR, WIDTH), bf16),
        pltpu.VMEM((3 * TR, WIDTH), bf16),
        pltpu.VMEM((4 * WIDTH, WIDTH), f32),
        pltpu.VMEM((4 * WIDTH, WIDTH), bf16),
        pltpu.VMEM((4 * WIDTH, WIDTH), bf16),
        pltpu.VMEM((TR, 4 * WIDTH), bf16),
        pltpu.VMEM((TR, 4 * WIDTH), bf16),
        pltpu.VMEM((ROWS, WIDTH), f32),
        dma((3,)), dma((4,)), dma((4,)),
        dma((2, 3, CH)), dma((2, 3, CH)),
        dma((4, 3)), dma((4, 3)),
        dma((3, 4)), dma((3, 4)),
    ]
    smem, hbm = pl.BlockSpec(memory_space=pltpu.SMEM), pl.BlockSpec(memory_space=pl.ANY)
    return pl.pallas_call(
        functools.partial(kernel, bits),
        out_shape=jax.ShapeDtypeStruct((ROWS, WIDTH), f32),
        in_specs=[smem] * 4 + [hbm] * 4,
        out_specs=hbm,
        scratch_shapes=scratch,
        compiler_params=pltpu.CompilerParams(
            collective_id=number, has_side_effects=True, vmem_limit_bytes=60 << 20
        ),
        name="filter_" + "".join(map(str, bits)),
    )


def local(
    vectors, local_blocks, local_cols, coupling_blocks, coupling_cols, partners, bounds, rotation
):
    total = partners[0, 0] + partners[1, 0] + partners[2, 0]
    index = sum((total > t).astype(jnp.int32) for t in TOTALS[:-1])
    return lax.switch(
        index,
        [fused(bits, number) for number, bits in enumerate(COMBOS)],
        local_cols, coupling_cols.transpose(0, 2, 1), partners, bounds, vectors,
        local_blocks.reshape(BC * KL, BLK, BLK),
        coupling_blocks.reshape(3, BC * KC, BLK, BLK),
        rotation,
    )


def solution(mesh):
    in_specs = (
        P("rows", "bands"),
        P("rows", None, None, None),
        P("rows", None),
        P(None, "rows", None, None, None),
        P(),
        P(),
        P(),
        P(),
    )
    out_specs = P("rows", "bands")
    return jax.shard_map(local, mesh=mesh, in_specs=in_specs, out_specs=out_specs, check_vma=False)
```

```python
import functools
import itertools

import jax
import jax.numpy as jnp
from jax import lax
from jax.experimental import pallas as pl
from jax.experimental.pallas import tpu as pltpu
from jax.sharding import PartitionSpec as P

MESH = pl.DeviceIdType.MESH
f32, bf16 = jnp.float32, jnp.bfloat16
ROWS, WIDTH, BLK = 1024, 256, 128
BC = ROWS // BLK
KL, KC = 6, 2
CH = 8
TR = 256
COMBOS = sorted(itertools.combinations(range(5), 3), key=lambda bits: sum(1 << b for b in bits))
TOTALS = [sum(1 << b for b in bits) for bits in COMBOS]


def flip(index, mask):
    bit, out = 1, index
    while bit <= mask:
        if mask & bit:
            out = out + bit * (1 - 2 * lax.rem(lax.div(index, bit), 2))
        bit *= 2
    return out


def dot(a, b):
    return jnp.dot(a, b, preferred_element_type=f32)


def split(x):
    hi = x.astype(bf16)
    return hi, (x - hi.astype(f32)).astype(bf16)


def rows_of(m, size):
    return pl.ds(pl.multiple_of(m * size, size), size)


def kernel(
    bits, local_cols, couple_cols, partners, bounds, v_hbm, local_hbm, couple_hbm, rot_hbm, out_hbm,
    v_own, own, mate, acc, other, own_blocks, turned, couple, outgoing, mate_blocks, h_local, h_couple,
    src_hi, src_lo, mate_hi, mate_lo, rot, rot_hi, rot_lo, part_hi, part_lo, out_v,
    in_sem, rot_sem, out_sem, send, recv, b_send, b_recv, g_send, g_recv,
):
    row, band = lax.axis_index("rows"), lax.axis_index("bands")
    relay = None
    for low, high in ((0, 1), (3, 4)):
        if low in bits and high in bits:
            relay = (1, 2)
            bits = tuple(b for b in bits if b not in (low, high)) + (low, high)
    masks = [1 << b for b in bits]
    direct = [p for p in range(3) if relay is None or p != relay[1]]
    beside = bits.index(2) if 2 in bits else None
    shared = (beside,) if beside is not None else (2,)
    mates = [(flip(row, m), band) for m in masks]
    twin = (row, flip(band, 1))
    across = (row, flip(band, 2))
    peers = mates + [twin, across]
    if beside is not None:
        aslant = (flip(row, 4), flip(band, 2))
        peers.append(aslant)
    if relay is not None:
        onward = (flip(row, masks[relay[0]] | masks[relay[1]]), band)
        peers.append(onward)

    def remote(src, dst, send_sem, recv_sem, to):
        return pltpu.make_async_remote_copy(
            src_ref=src, dst_ref=dst, send_sem=send_sem, recv_sem=recv_sem, device_id=to, device_id_type=MESH
        )

    loads = [
        pltpu.make_async_copy(couple_hbm, couple, in_sem.at[0]),
        pltpu.make_async_copy(local_hbm, own_blocks, in_sem.at[1]),
        pltpu.make_async_copy(v_hbm, v_own, in_sem.at[2]),
    ]
    for load in loads:
        load.start()
    rot_loads = []
    for g in range(4):
        piece = rot_hbm.at[rows_of(flip(band, g), WIDTH), rows_of(band, WIDTH)]
        rot_loads.append(pltpu.make_async_copy(piece, rot.at[pl.ds(g * WIDTH, WIDTH)], rot_sem.at[g]))
        rot_loads[-1].start()

    barrier = pltpu.get_barrier_semaphore()
    for peer in peers:
        pl.semaphore_signal(barrier, inc=1, device_id=peer, device_id_type=MESH)
    pl.semaphore_wait(barrier, len(peers))

    def chunk(ph, p, c):
        rs = rows_of(c, BLK)
        if p in direct:
            source, to = own.at[ph], mates[p]
        else:
            source, to = mate.at[ph, relay[0]], onward
        return remote(source.at[rs], mate.at[ph, p, rs], send.at[ph, p, c], recv.at[ph, p, c], to)

    def pass_on(ph, c):
        if relay is not None:
            chunk(ph, relay[0], c).wait_recv()
            chunk(ph, relay[1], c).start()

    def hand(kind, m):
        rs = rows_of(m, TR)
        source = other.at[1] if kind == 2 else v_hbm
        return remote(
            source.at[rs], other.at[kind, rs], g_send.at[kind, m], g_recv.at[kind, m], across if kind == 1 else twin
        )

    hand(1, 0).start()
    hand(0, 0).start()

    colours = []
    for m in masks:
        colour = jnp.int32(0)
        for c in (1, 2):
            colour = colour + jnp.where(partners[c, 0] == m, c, 0)
        colours.append(colour)

    counts = [BC * KC // (4 if p in shared else 2) for p in range(3)]
    firsts = [counts[p] * (band if p in shared else lax.rem(band, 2)) for p in range(3)]
    loads[0].wait()
    blocks = []
    for p in range(3):
        count, first = counts[p], firsts[p]

        @pl.loop(0, count // 2)
        def _(q, p=p, first=first):
            for u in range(2):
                outgoing[p, q * 2 + u] = couple[colours[p], first + q * 2 + u]

        blocks.append(
            remote(
                outgoing.at[p, pl.ds(0, count)], mate_blocks.at[p, pl.ds(first, count)],
                b_send.at[0, p], b_recv.at[0, p], mates[p],
            )
        )
        blocks[-1].start()
        if p == beside:
            to_aslant = remote(
                outgoing.at[p, pl.ds(0, count)], mate_blocks.at[p, pl.ds(first, count)],
                b_send.at[2, p], b_recv.at[2, p], aslant,
            )
            to_aslant.start()

    @pl.loop(1, ROWS // TR - (1 if beside is None else 0))
    def _(m):
        hand(1, m).start()
        hand(0, m).start()

    def turn(source, number):
        @pl.loop(0, number // 4)
        def _(q):
            for u in range(4):
                turned[q * 4 + u] = source[q * 4 + u].T

    def one_if(flag):
        return jnp.where(flag, 1.0, 0.0).astype(f32)

    def added(terms):
        return functools.reduce(lambda a, b: a + b, terms)

    def build_local():
        @pl.loop(0, BC)
        def _(i):
            rs = rows_of(i, BLK)

            @pl.loop(0, BC // 2)
            def _(q):
                for u in range(2):
                    j = q * 2 + u
                    total = added(
                        [own_blocks[i * KL + k] * one_if(local_cols[i, k] == j) for k in range(KL)]
                        + [turned[j * KL + k] * one_if(local_cols[j, k] == i) for k in range(KL)]
                    )
                    hi, lo = split(total)
                    h_local[rs, rows_of(j, BLK)] = hi
                    h_local[rs, rows_of(BC + j, BLK)] = lo

    def rotate(m):
        rs = rows_of(m, TR)
        hand(1, m).wait_recv()
        hand(2, m).start()
        hand(0, m).wait_recv()
        part_hi[:, :WIDTH], part_lo[:, :WIDTH] = split(v_own[rs])
        for g in (1, 2, 3):
            if g == 3:
                hand(2, m).wait_recv()
            gs = slice(g * WIDTH, (g + 1) * WIDTH)
            part_hi[:, gs], part_lo[:, gs] = split(other[g - 1, rs])
        turned_bands = (
            dot(part_hi[...], rot_hi[...]) + dot(part_lo[...], rot_hi[...]) + dot(part_hi[...], rot_lo[...])
        )
        own[0, rs] = turned_bands
        for e in range(2):
            for p in direct:
                chunk(0, p, 2 * m + e).start()
        src_hi[rs], src_lo[rs] = split(turned_bands)

    def forward(kind, p, at, to):
        span = mate_blocks.at[p, pl.ds(at, counts[p])]
        return remote(span, span, b_send.at[kind, p], b_recv.at[kind, p], to)

    to_twin = [forward(1, p, firsts[p], twin) for p in range(3)]
    to_across = {p: to_aslant if p == beside else forward(2, p, firsts[p], across) for p in shared}
    far_to_twin = {p: forward(3, p, counts[p] * flip(band, 2), twin) for p in shared}

    for load in rot_loads:
        load.wait()

    @pl.loop(0, 4)
    def _(g):
        rs = rows_of(g, WIDTH)
        rot_hi[rs], rot_lo[rs] = split(rot[rs])

    loads[1].wait()
    loads[2].wait()

    def build_couple(p):
        def pick(values):
            return jnp.where(p == 0, values[0], jnp.where(p == 1, values[1], values[2]))

        colour = pick(colours)
        here, there = row * BC, pick([m[0] for m in mates]) * BC

        for k in range(3):
            @pl.when(p == k)
            def _(k=k):
                if k in shared:
                    to_across[k].wait_recv()
                    far_to_twin[k].start()
                to_twin[k].wait_recv()
                if k in shared:
                    far_to_twin[k].wait_recv()

        turn(mate_blocks.at[p], BC * KC)

        @pl.loop(0, BC)
        def _(i):
            rs = rows_of(i, BLK)

            @pl.loop(0, BC // 2)
            def _(q):
                for u in range(2):
                    j = q * 2 + u
                    total = added(
                        [
                            couple[colour, i * KC + k] * one_if(couple_cols[colour, k, here + i] == j)
                            for k in range(KC)
                        ]
                        + [
                            turned[j * KC + k] * one_if(couple_cols[colour, k, there + j] == i)
                            for k in range(KC)
                        ]
                    )
                    hi, lo = split(total)
                    at = p * 2 + u
                    h_couple[q, rs, rows_of(at, BLK)] = hi
                    h_couple[q, rs, rows_of(6 + at, BLK)] = lo

        if relay is not None and beside is not None:
            pass_on(0, 2 * p)
            pass_on(0, 2 * p + 1)
        elif relay is not None:
            @pl.when(p < 2)
            def _():
                pass_on(0, p)

            @pl.when(p == 1)
            def _():
                pass_on(0, 2)

    @pl.loop(0, 5)
    def _(step):
        @pl.when(step == 0)
        def _():
            turn(own_blocks, BC * KL)

        @pl.when(step == 1)
        def _():
            build_local()
            for p in (1, 2, 0):
                blocks[p].wait_recv()
                if p in shared and p != beside:
                    to_across[p].start()
                to_twin[p].start()
            if beside is None:
                hand(1, 3).start()
                hand(0, 3).start()

        @pl.when(step >= 2)
        def _():
            build_couple(step - 2)

        late = 4 if relay is None or beside is None else 3

        @pl.when((step < 3) | (step == late))
        def _():
            rotate(step - jnp.where(step == 4, 1, 0))

    if beside is None:
        pass_on(0, 3)
        pass_on(0, 4)

    def couple_product(kc, rs):
        return (
            dot(h_couple[kc, rs, :3 * TR], mate_hi[...])
            + dot(h_couple[kc, rs, 3 * TR:], mate_hi[...])
            + dot(h_couple[kc, rs, :3 * TR], mate_lo[...])
        )

    def receive(ph, kc):
        if relay is not None:
            @pl.when((ph == 1) & (kc == 0))
            def _():
                pass_on(1, 0)
                pass_on(1, 1)

            @pl.when((ph == 1) & (kc < 3))
            def _():
                pass_on(1, 2 * kc + 2)
                pass_on(1, 2 * kc + 3)

            @pl.when((ph == 0) & (kc < 2))
            def _():
                pass_on(0, kc + (5 if beside is None else 6))

            if beside is None:
                @pl.when((ph == 0) & (kc == 1))
                def _():
                    pass_on(0, 7)

        for e in range(2):
            for p in range(3):
                if relay is None or p != relay[0]:
                    chunk(ph, p, 2 * kc + e).wait_recv()
        for p in range(3):
            hi, lo = split(mate[ph, p, rows_of(kc, TR)])
            mate_hi[p * TR:(p + 1) * TR] = hi
            mate_lo[p * TR:(p + 1) * TR] = lo

    wide = (1, WIDTH)
    lowest, lower, upper = (jnp.full(wide, bounds[i], f32) for i in range(3))
    half_width = (upper - lower) / 2.0
    centre = (upper + lower) / 2.0
    sigma_one = half_width / (lowest - centre)
    sigma_two = 1.0 / (2.0 / sigma_one - sigma_one)

    def store(m):
        rs = rows_of(m, TR)
        return pltpu.make_async_copy(out_v.at[rs], out_hbm.at[rs], out_sem.at[m])

    @pl.loop(0, 2)
    def _(ph):
        @pl.loop(0, ROWS // TR)
        def _(m):
            rs = rows_of(m, TR)
            acc[rs] = (
                dot(h_local[rs, :ROWS], src_hi[...])
                + dot(h_local[rs, ROWS:], src_hi[...])
                + dot(h_local[rs, :ROWS], src_lo[...])
            )

        @pl.loop(0, 3)
        def _(kc):
            receive(ph, kc)

            @pl.loop(0, ROWS // TR)
            def _(m):
                rs = rows_of(m, TR)
                acc[rs] += couple_product(kc, rs)

        receive(ph, jnp.int32(3))
        outer = jnp.where(ph == 0, sigma_one, 2.0 * sigma_two) / half_width
        back = jnp.where(ph == 0, 0.0, sigma_one * sigma_two)

        @pl.loop(0, ROWS // TR)
        def _(m):
            rs = rows_of(m, TR)
            total = acc[rs] + couple_product(3, rs)
            result = (total - centre * own[ph, rs]) * outer - back * own[0, rs]

            @pl.when(ph == 0)
            def _():
                own[1, rs] = result
                for e in range(2):
                    for p in direct:
                        chunk(1, p, 2 * m + e).start()
                src_hi[rs], src_lo[rs] = split(result)

            @pl.when(ph == 1)
            def _():
                out_v[rs] = result
                store(m).start()

    @pl.loop(0, CH)
    def _(c):
        for ph in range(2):
            for p in range(3):
                chunk(ph, p, c).wait_send()

    for copy in blocks + to_twin + list(to_across.values()) + list(far_to_twin.values()):
        copy.wait_send()

    @pl.loop(0, ROWS // TR)
    def _(m):
        for kind in range(3):
            hand(kind, m).wait_send()
        store(m).wait()


def fused(bits, number):
    dma = pltpu.SemaphoreType.DMA
    scratch = [
        pltpu.VMEM((ROWS, WIDTH), f32),
        pltpu.VMEM((2, ROWS, WIDTH), f32),
        pltpu.VMEM((2, 3, ROWS, WIDTH), f32),
        pltpu.VMEM((ROWS, WIDTH), f32),
        pltpu.VMEM((3, ROWS, WIDTH), f32),
        pltpu.VMEM((BC * KL, BLK, BLK), f32),
        pltpu.VMEM((BC * KL, BLK, BLK), f32),
        pltpu.VMEM((3, BC * KC, BLK, BLK), f32),
        pltpu.VMEM((3, BC * KC // 2, BLK, BLK), f32),
        pltpu.VMEM((3, BC * KC, BLK, BLK), f32),
        pltpu.VMEM((ROWS, 2 * ROWS), bf16),
        pltpu.VMEM((4, ROWS, 6 * TR), bf16),
        pltpu.VMEM((ROWS, WIDTH), bf16),
        pltpu.VMEM((ROWS, WIDTH), bf16),
        pltpu.VMEM((3 * TR, WIDTH), bf16),
        pltpu.VMEM((3 * TR, WIDTH), bf16),
        pltpu.VMEM((4 * WIDTH, WIDTH), f32),
        pltpu.VMEM((4 * WIDTH, WIDTH), bf16),
        pltpu.VMEM((4 * WIDTH, WIDTH), bf16),
        pltpu.VMEM((TR, 4 * WIDTH), bf16),
        pltpu.VMEM((TR, 4 * WIDTH), bf16),
        pltpu.VMEM((ROWS, WIDTH), f32),
        dma((3,)), dma((4,)), dma((4,)),
        dma((2, 3, CH)), dma((2, 3, CH)),
        dma((4, 3)), dma((4, 3)),
        dma((3, 4)), dma((3, 4)),
    ]
    smem, hbm = pl.BlockSpec(memory_space=pltpu.SMEM), pl.BlockSpec(memory_space=pl.ANY)
    return pl.pallas_call(
        functools.partial(kernel, bits),
        out_shape=jax.ShapeDtypeStruct((ROWS, WIDTH), f32),
        in_specs=[smem] * 4 + [hbm] * 4,
        out_specs=hbm,
        scratch_shapes=scratch,
        compiler_params=pltpu.CompilerParams(
            collective_id=number, has_side_effects=True, vmem_limit_bytes=60 << 20
        ),
        name="filter_" + "".join(map(str, bits)),
    )


def local(
    vectors, local_blocks, local_cols, coupling_blocks, coupling_cols, partners, bounds, rotation
):
    total = partners[0, 0] + partners[1, 0] + partners[2, 0]
    index = sum((total > t).astype(jnp.int32) for t in TOTALS[:-1])
    return lax.switch(
        index,
        [fused(bits, number) for number, bits in enumerate(COMBOS)],
        local_cols, coupling_cols.transpose(0, 2, 1), partners, bounds, vectors,
        local_blocks.reshape(BC * KL, BLK, BLK),
        coupling_blocks.reshape(3, BC * KC, BLK, BLK),
        rotation,
    )


def solution(mesh):
    in_specs = (
        P("rows", "bands"),
        P("rows", None, None, None),
        P("rows", None),
        P(None, "rows", None, None, None),
        P(),
        P(),
        P(),
        P(),
    )
    out_specs = P("rows", "bands")
    return jax.shard_map(local, mesh=mesh, in_specs=in_specs, out_specs=out_specs, check_vma=False)
```
